32 devices in a mesh: groups: 2 (over y), rows: 8 (over z, x), sub: 2 (over core).
Axes of the slice: x: 2, y: 2, z: 4, core: 2. Of those that a mesh axis runs over, the one named last changes fastest.
Arguments:
- residuals: bfloat16 [2048, 2048], P(('groups', 'rows'), 'sub'), parts along dimension 0, may hold values from -96 to 96
- codes: int32 [2048, 256], P(('groups', 'rows'), 'sub'), parts along dimension 0, may hold values from 0 to 127
- codebook: float32 [512, 8, 128], P(('groups', 'sub')), parts along dimension 0, may hold values from -4 to 4
Outputs:
- refined: float32 [512, 8, 128], P(('groups', 'sub')), parts along dimension 0
The draws below stay inside these ranges and needn't reach their ends.
There are 2 independent parts, one for each index of `groups`. The reference program is written for one: setup_inputs(seed, part) draws one part's arguments, and reference() takes and returns one part's arrays. A program takes and returns all parts, laid end to end along the dimension named above; each array names one. Nothing has to cross between parts.
All inputs are finite; a program needn't handle non-finite values.
Results may differ from the reference program's by a relative error of at most 0.0037.
Values sent between devices are 32-bit elements; how exact they have to be, the bound alone decides.
A program may use at most 64 MiB of HBM per device.

```python
import jax
import jax.numpy as jnp
from jax import lax

SUBSPACES = 256
SUBDIM = 8
CODEWORDS = 128
VECTORS = 1024


def true_codes(key):
    return jax.random.randint(jax.random.fold_in(jax.random.fold_in(key, 11), 2), (VECTORS, SUBSPACES), 0, CODEWORDS, dtype=jnp.int32)


def draw_codes(key, part):
    truth = true_codes(key)
    base = jax.random.fold_in(key, 12)
    swapped = jax.random.randint(jax.random.fold_in(base, 1), (VECTORS, SUBSPACES), 0, 10, dtype=jnp.int32) < 3
    other = jax.random.randint(jax.random.fold_in(base, 2), (VECTORS, SUBSPACES), 0, CODEWORDS, dtype=jnp.int32)
    return jnp.where(swapped, other, truth)


def draw_residuals(key, part):
    truth = true_codes(key)
    centers = jax.random.truncated_normal(jax.random.fold_in(jax.random.fold_in(key, 11), 1), -3.0, 3.0, (SUBSPACES, CODEWORDS, SUBDIM), jnp.float32)
    picked = centers[jnp.arange(SUBSPACES, dtype=jnp.int32)[None, :], truth]
    noise = jax.random.truncated_normal(jax.random.fold_in(key, 21), -3.0, 3.0, (VECTORS, SUBSPACES, SUBDIM), jnp.float32)
    vectors = picked + noise
    return vectors.reshape(VECTORS, SUBSPACES * SUBDIM).astype(jnp.bfloat16)


def block_scale(own_key, shape, split, least, largest):
    factor_of = 1.0
    for position, shards_of in split:
        steps = jax.random.uniform(jax.random.fold_in(jax.random.fold_in(own_key, 6), position), (shards_of,), jnp.float32, least / len(split), largest / len(split))
        factor_of = factor_of * jnp.repeat(jnp.exp(steps), shape[position] // shards_of).reshape((-1,) + (1,) * (len(shape) - 1 - position))
    return factor_of


def gaussian(stream_key, shape, width, bound, pieces=(), held_as=jnp.bfloat16):
    result = jax.random.normal(stream_key, shape, jnp.float32) * width
    if len(pieces) > 0:
        result = block_scale(stream_key, shape, pieces, -0.22, 0.18) * result
    return jnp.clip(result, min=-bound, max=bound).astype(held_as)


def setup_inputs(seed: int = 0, part: int = 0) -> dict:
    seeds = jax.random.split(jax.random.key(seed), 4)
    part_keys = jax.random.split(jax.random.fold_in(seeds[3], part), 4)
    return {
        "residuals": draw_residuals(jax.random.fold_in(jax.random.fold_in(seeds[3], part), 71), part),
        "codes": draw_codes(jax.random.fold_in(jax.random.fold_in(seeds[3], part), 71), part),
        "codebook": gaussian(part_keys[2], (SUBSPACES, SUBDIM, CODEWORDS), 1.0, 4.0, ((0, 2),), jnp.float32),
    }


def renew(prior, sums, counts, lam):
    return (sums + lam * prior) / (counts[:, None, :] + lam)


def reference(residuals, codes, codebook):
    lam = VECTORS / (8.0 * CODEWORDS)
    levels = jnp.arange(CODEWORDS, dtype=jnp.int32)
    index = jnp.arange(SUBSPACES, dtype=jnp.int32)

    def first(m):
        cols = lax.dynamic_slice_in_dim(residuals, m * SUBDIM, SUBDIM, 1).astype(jnp.float32)
        column = lax.dynamic_slice_in_dim(codes, m, 1, 1)
        onehot = (column == levels[None, :]).astype(jnp.float32)
        sums = jnp.dot(cols.T, onehot, precision=lax.Precision.HIGHEST, preferred_element_type=jnp.float32)
        return sums, jnp.sum(onehot, axis=0)

    sums1, counts1 = lax.map(first, index)
    book1 = renew(codebook, sums1, counts1, lam)

    def second(m):
        cols = lax.dynamic_slice_in_dim(residuals, m * SUBDIM, SUBDIM, 1)
        center = book1[m]
        cross = jnp.dot(cols, center.astype(jnp.bfloat16), preferred_element_type=jnp.float32)
        scores = 2.0 * cross - jnp.sum(center * center, axis=0)[None, :]
        weights = jax.nn.softmax(scores, axis=1).astype(jnp.bfloat16)
        sums = jnp.dot(cols.T, weights, preferred_element_type=jnp.float32)
        return sums, jnp.sum(weights.astype(jnp.float32), axis=0)

    sums2, counts2 = lax.map(second, index)
    return renew(book1, sums2, counts2, lam)
```

```python
import functools

import jax
import jax.numpy as jnp
from jax import lax
from jax.experimental import pallas as pl
from jax.experimental.pallas import tpu as pltpu
from jax.sharding import PartitionSpec as P


def kernel(n, gs, groups, lam, tile, x_ref, c_ref, cb_ref, o_ref,
           xs, xr, cb, res, send_x, recv_x, send_o, recv_o, own, cb_sem):
    rows, width = x_ref.shape[0], cb_ref.shape[-1]
    me = lax.axis_index("rows")
    subdim = cb_ref.shape[2] // gs
    per = gs * groups
    span = gs * subdim

    barrier = pltpu.get_barrier_semaphore()

    def greet(k, _):
        pl.semaphore_signal(barrier, inc=1, device_id={"rows": lax.rem(me + k, n)},
                            device_id_type=pl.DeviceIdType.MESH)
        return 0

    lax.fori_loop(1, n, greet, 0)
    prior = pltpu.make_async_copy(cb_ref.at[me], cb, cb_sem)
    prior.start()

    flipped = x_ref[...].astype(jnp.float32).T
    labels = c_ref[...].astype(jnp.float32).T
    for j in range(n):
        for g in range(groups):
            at = j * per + g * gs
            xs[j, g, :span, :] = flipped[at * subdim:at * subdim + span]
            xs[j, g, span:span + gs, :] = labels[at:at + gs]
    xr[me] = xs[me]
    pl.semaphore_wait(barrier, n - 1)

    def block(source, target, g, slot):
        return pltpu.make_async_remote_copy(
            src_ref=xs.at[target, g], dst_ref=xr.at[source, g],
            send_sem=send_x.at[g, target], recv_sem=recv_x.at[g, slot],
            device_id={"rows": target}, device_id_type=pl.DeviceIdType.MESH)

    def result(source, target, g, slot):
        return pltpu.make_async_remote_copy(
            src_ref=res.at[g], dst_ref=o_ref.at[source, g],
            send_sem=send_o.at[g, target], recv_sem=recv_o.at[g, slot],
            device_id={"rows": target}, device_id_type=pl.DeviceIdType.MESH)

    def each_peer(act):
        def body(k, _):
            act(lax.rem(me + k, n))
            return 0
        lax.fori_loop(1, n, body, 0)

    for g in range(groups):
        each_peer(lambda p, g=g: block(me, p, g, me).start())
    prior.wait()

    level = lax.broadcasted_iota(jnp.int32, (width, tile * rows), 0).astype(jnp.float32)
    ones = jnp.ones((8, tile * rows), jnp.float32)

    def over_tiles(step):
        if n == tile:
            return step(0)
        return lax.fori_loop(
            0, n // tile, lambda t, total: total + step(t),
            jnp.zeros((subdim + 8, width), jnp.float32))

    for g in range(groups):
        each_peer(lambda p, g=g: block(p, p, g, p).wait_recv())

        def train(m, _, g=g):
            line = pl.multiple_of(m * subdim, subdim)

            def columns(t):
                parts = [xr[t * tile + s, g, pl.ds(line, subdim), :] for s in range(tile)]
                full = jnp.concatenate(parts, axis=1)
                return jnp.concatenate([full, ones], axis=0).astype(jnp.bfloat16)

            def reduce_rows(points, weights):
                return lax.dot_general(points, weights, (((1,), (1,)), ((), ())),
                                       preferred_element_type=jnp.float32)

            def first(t):
                code = jnp.concatenate(
                    [xr[t * tile + s, g, pl.ds(span + m, 1), :] for s in range(tile)], axis=1)
                onehot = (level == code).astype(jnp.float32).astype(jnp.bfloat16)
                return reduce_rows(columns(t), onehot)

            total = over_tiles(first)
            before = cb[g, pl.ds(line, subdim), :]
            book = (total[:subdim] + lam * before) / (total[subdim:subdim + 1] + lam)
            norm = -jnp.sum(book * book, axis=0, keepdims=True)
            high = norm.astype(jnp.bfloat16).astype(jnp.float32)
            middle = (norm - high).astype(jnp.bfloat16).astype(jnp.float32)
            low = norm - high - middle
            center = jnp.concatenate(
                [2.0 * book.astype(jnp.bfloat16).astype(jnp.float32), high, middle, low,
                 jnp.zeros((5, width), jnp.float32)], axis=0).T.astype(jnp.bfloat16)

            def second(t):
                points = columns(t)
                scores = jnp.dot(center, points, preferred_element_type=jnp.float32)
                top = jnp.max(scores, axis=0, keepdims=True)
                raised = jnp.exp(scores - top)
                share = 1.0 / jnp.sum(raised, axis=0, keepdims=True)
                return reduce_rows(points, (raised * share).astype(jnp.bfloat16))

            total = over_tiles(second)
            res[g, pl.ds(line, subdim), :] = (
                (total[:subdim] + lam * book) / (total[subdim:subdim + 1] + lam))
            return 0

        lax.fori_loop(0, gs, train, 0)
        each_peer(lambda p, g=g: result(me, p, g, me).start())
        pltpu.make_async_copy(res.at[g], o_ref.at[me, g], own.at[g]).start()

    for g in range(groups):
        each_peer(lambda p, g=g: block(me, p, g, me).wait_send())
        each_peer(lambda p, g=g: result(me, p, g, me).wait_send())
        each_peer(lambda p, g=g: result(p, p, g, p).wait_recv())
        pltpu.make_async_copy(res.at[g], o_ref.at[me, g], own.at[g]).wait()


def shards(residuals, codes, codebook):
    rows = residuals.shape[0]
    local, subdim, width = codebook.shape
    n = lax.axis_size("rows")
    per = local // n
    gs = 8 if per % 8 == 0 else per
    groups = per // gs
    lam = rows * n / (8.0 * width)
    tile = min(n, 8)
    span = gs * subdim
    lines = span + -(-gs // 8) * 8
    shape = (n, groups, span, width)
    out = pl.pallas_call(
        functools.partial(kernel, n, gs, groups, lam, tile),
        out_shape=jax.ShapeDtypeStruct(shape, jnp.float32),
        in_specs=[pl.BlockSpec(memory_space=pltpu.VMEM)] * 2 + [pl.BlockSpec(memory_space=pl.ANY)],
        out_specs=pl.BlockSpec(memory_space=pl.ANY),
        scratch_shapes=[
            pltpu.VMEM((n, groups, lines, rows), jnp.float32),
            pltpu.VMEM((n, groups, lines, rows), jnp.float32),
            pltpu.VMEM((groups, span, width), jnp.float32),
            pltpu.VMEM((groups, span, width), jnp.float32),
            pltpu.SemaphoreType.DMA((groups, n)),
            pltpu.SemaphoreType.DMA((groups, n)),
            pltpu.SemaphoreType.DMA((groups, n)),
            pltpu.SemaphoreType.DMA((groups, n)),
            pltpu.SemaphoreType.DMA((groups,)),
            pltpu.SemaphoreType.DMA,
        ],
        compiler_params=pltpu.CompilerParams(collective_id=0, has_side_effects=True),
        name="lloyd",
    )(residuals, codes, codebook.reshape(shape))
    return out.reshape(local, subdim, width)


def solution(mesh):
    in_specs = (
        P(("groups", "rows"), "sub"),
        P(("groups", "rows"), "sub"),
        P(("groups", "sub"), None, None),
    )
    out_specs = P(("groups", "sub"), None, None)
    return jax.shard_map(shards, mesh=mesh, in_specs=in_specs, out_specs=out_specs, check_vma=False)
```

```python
import functools

import jax
import jax.numpy as jnp
from jax import lax
from jax.experimental import pallas as pl
from jax.experimental.pallas import tpu as pltpu
from jax.sharding import PartitionSpec as P

MESH = pl.DeviceIdType.MESH


def kernel(n, sizes, direct, lam, tile, x_hbm, c_hbm, cb_hbm, o_ref, x_ref, c_ref,
           xs, xr, cb, res, send_x, recv_x, send_o, recv_o, relay, own, in_sem):
    rows, width = x_ref.shape[0], cb.shape[-1]
    per = sum(sizes)
    subdim = cb.shape[0] // per
    base = xs.shape[1] - per * subdim
    starts = [sum(sizes[:g]) for g in range(len(sizes))]
    groups = range(len(sizes))
    side = 2 if n % 2 == 0 else 1
    levels = n // side
    me = lax.axis_index("rows")
    level, column = lax.div(me, side), lax.rem(me, side)

    barrier = pltpu.get_barrier_semaphore()

    def greet(k, _):
        pl.semaphore_signal(barrier, inc=1, device_id={"rows": lax.rem(me + k, n)},
                            device_id_type=MESH)
        return 0

    lax.fori_loop(1, n, greet, 0, unroll=n <= 8)
    loads = [pltpu.make_async_copy(x_hbm, x_ref, in_sem.at[0]),
             pltpu.make_async_copy(c_hbm, c_ref, in_sem.at[1]),
             pltpu.make_async_copy(cb_hbm.at[me], cb, in_sem.at[2])]
    for load in loads:
        load.start()
    loads[0].wait()
    flipped = x_ref[...].astype(jnp.float32).T
    for j in range(n):
        at = j * per * subdim
        xs[j, base:, :] = flipped[at:at + per * subdim]
    loads[1].wait()
    labels = c_ref[...].astype(jnp.float32).T
    for j in range(n):
        xs[j, :per, :] = labels[j * per:(j + 1) * per]
        if base > per:
            xs[j, per:base, :] = jnp.zeros((base - per, rows), jnp.float32)
    xr[me] = xs[me]
    loads[2].wait()
    pl.semaphore_wait(barrier, n - 1)

    def piece(g):
        first = 0 if g == 0 else base + starts[g] * subdim
        return pl.ds(first, base + (starts[g] + sizes[g]) * subdim - first)

    def lines(g):
        return pl.ds(starts[g] * subdim, sizes[g] * subdim)

    def block(source, target, g):
        return pltpu.make_async_remote_copy(
            src_ref=xs.at[target, piece(g)], dst_ref=xr.at[source, piece(g)],
            send_sem=send_x.at[g, target], recv_sem=recv_x.at[g, source],
            device_id={"rows": target}, device_id_type=MESH)

    def result(source, target, g):
        return pltpu.make_async_remote_copy(
            src_ref=res.at[lines(g)], dst_ref=o_ref.at[source, lines(g)],
            send_sem=send_o.at[g, target], recv_sem=recv_o.at[g, source],
            device_id={"rows": target}, device_id_type=MESH)

    def passed(source, g):
        return pltpu.make_async_remote_copy(
            src_ref=o_ref.at[source, lines(g)], dst_ref=o_ref.at[source, lines(g)],
            send_sem=relay.at[g, source], recv_sem=recv_o.at[g, source],
            device_id={"rows": level * side + 1 - column}, device_id_type=MESH)

    def kept(g):
        return pltpu.make_async_copy(res.at[lines(g)], o_ref.at[me, lines(g)], own.at[g])

    def each_peer(act):
        def body(k, _):
            act(lax.rem(me + k, n))
            return 0
        lax.fori_loop(1, n, body, 0, unroll=n <= 8)

    def each_level(first, where, act):
        def body(k, _):
            act(lax.rem(level + k, levels) * side + where)
            return 0
        lax.fori_loop(first, levels, body, 0, unroll=n <= 8)

    for g in groups:
        each_peer(lambda p, g=g: block(me, p, g).start())

    number = lax.broadcasted_iota(jnp.int32, (width, tile * rows), 0).astype(jnp.float32)
    ones = jnp.ones((8, tile * rows), jnp.float32)

    def over_tiles(step):
        if n == tile:
            return step(0)
        return lax.fori_loop(
            0, n // tile, lambda t, total: total + step(t),
            jnp.zeros((subdim + 8, width), jnp.float32))

    def reduce_rows(points, weights):
        return lax.dot_general(points, weights, (((1,), (1,)), ((), ())),
                               preferred_element_type=jnp.float32)

    def train(m, _):
        line = pl.multiple_of(m * subdim, subdim)

        def columns(t):
            parts = [xr[t * tile + s, pl.ds(base + line, subdim), :] for s in range(tile)]
            full = jnp.concatenate(parts, axis=1)
            return jnp.concatenate([full, ones], axis=0).astype(jnp.bfloat16)

        def first(t):
            code = jnp.concatenate(
                [xr[t * tile + s, pl.ds(m, 1), :] for s in range(tile)], axis=1)
            onehot = (number == code).astype(jnp.float32).astype(jnp.bfloat16)
            return reduce_rows(columns(t), onehot)

        total = over_tiles(first)
        before = cb[pl.ds(line, subdim), :]
        book = (total[:subdim] + lam * before) / (total[subdim:subdim + 1] + lam)
        norm = -jnp.sum(book * book, axis=0, keepdims=True)
        high = norm.astype(jnp.bfloat16).astype(jnp.float32)
        middle = (norm - high).astype(jnp.bfloat16).astype(jnp.float32)
        low = norm - high - middle
        center = jnp.concatenate(
            [2.0 * book.astype(jnp.bfloat16).astype(jnp.float32), high, middle, low,
             jnp.zeros((5, width), jnp.float32)], axis=0).T.astype(jnp.bfloat16)

        def second(t):
            points = columns(t)
            scores = jnp.dot(center, points, preferred_element_type=jnp.float32)
            top = jnp.max(scores, axis=0, keepdims=True)
            raised = jnp.exp(scores - top)
            share = 1.0 / jnp.sum(raised, axis=0, keepdims=True)
            return reduce_rows(points, (raised * share).astype(jnp.bfloat16))

        total = over_tiles(second)
        res[pl.ds(line, subdim), :] = (
            (total[:subdim] + lam * book) / (total[subdim:subdim + 1] + lam))
        return 0

    def forward(g):
        def one(source):
            result(source, source, g).wait_recv()
            passed(source, g).start()
        each_level(1, column, one)

    for g in groups:
        each_peer(lambda p, g=g: block(p, p, g).wait_recv())
        def several(i, _, g=g):
            for u in range(min(4, sizes[g])):
                train(starts[g] + i * min(4, sizes[g]) + u, 0)
            return 0
        lax.fori_loop(0, sizes[g] // min(4, sizes[g]), several, 0)
        if direct[g] or side == 1:
            each_peer(lambda p, g=g: result(me, p, g).start())
        else:
            each_level(1, column, lambda p, g=g: result(me, p, g).start())
            result(me, level * side + 1 - column, g).start()
        kept(g).start()
        if g > 0 and not direct[g - 1] and side == 2:
            forward(g - 1)
    if not direct[-1] and side == 2:
        forward(len(sizes) - 1)

    for g in groups:
        each_peer(lambda p, g=g: block(me, p, g).wait_send())
        if direct[g] or side == 1:
            each_peer(lambda p, g=g: result(me, p, g).wait_send())
            each_peer(lambda p, g=g: result(p, p, g).wait_recv())
        else:
            each_level(1, column, lambda p, g=g: result(me, p, g).wait_send())
            result(me, level * side + 1 - column, g).wait_send()
            each_level(1, column, lambda p, g=g: passed(p, g).wait_send())
            each_level(0, 1 - column, lambda p, g=g: result(p, p, g).wait_recv())
        kept(g).wait()


def shards(residuals, codes, codebook):
    rows = residuals.shape[0]
    local, subdim, width = codebook.shape
    n = lax.axis_size("rows")
    per = local // n
    parts = 4 if per % 4 == 0 else 1
    sizes = (per // parts,) * parts
    direct = (False,) * (parts - 1) + (True,)
    lam = rows * n / (8.0 * width)
    tile = min(n, 8)
    base = -(-per // 8) * 8
    held = base + per * subdim
    shape = (n, per * subdim, width)
    out = pl.pallas_call(
        functools.partial(kernel, n, sizes, direct, lam, tile),
        out_shape=pltpu.VMEM(shape, jnp.float32),
        in_specs=[pl.BlockSpec(memory_space=pl.ANY)] * 3,
        out_specs=pl.BlockSpec(memory_space=pltpu.VMEM),
        scratch_shapes=[
            pltpu.VMEM(residuals.shape, residuals.dtype),
            pltpu.VMEM(codes.shape, codes.dtype),
            pltpu.VMEM((n, held, rows), jnp.float32),
            pltpu.VMEM((n, held, rows), jnp.float32),
            pltpu.VMEM((per * subdim, width), jnp.float32),
            pltpu.VMEM((per * subdim, width), jnp.float32),
            pltpu.SemaphoreType.DMA((parts, n)),
            pltpu.SemaphoreType.DMA((parts, n)),
            pltpu.SemaphoreType.DMA((parts, n)),
            pltpu.SemaphoreType.DMA((parts, n)),
            pltpu.SemaphoreType.DMA((parts, n)),
            pltpu.SemaphoreType.DMA((parts,)),
            pltpu.SemaphoreType.DMA((3,)),
        ],
        compiler_params=pltpu.CompilerParams(collective_id=0, has_side_effects=True),
        name="lloyd",
    )(residuals, codes, codebook.reshape(shape))
    return out.reshape(local, subdim, width)


def solution(mesh):
    in_specs = (
        P(("groups", "rows"), "sub"),
        P(("groups", "rows"), "sub"),
        P(("groups", "sub"), None, None),
    )
    out_specs = P(("groups", "sub"), None, None)
    return jax.shard_map(shards, mesh=mesh, in_specs=in_specs, out_specs=out_specs, check_vma=False)
```

```python
import functools

import jax
import jax.numpy as jnp
from jax import lax
from jax.experimental import pallas as pl
from jax.experimental.pallas import tpu as pltpu
from jax.sharding import PartitionSpec as P

MESH = pl.DeviceIdType.MESH


def kernel(n, sizes, direct, lam, tile, x_hbm, c_hbm, cb_hbm, o_ref, x_ref, c_ref,
           xs, xr, cb, res, send_x, recv_x, send_o, recv_o, relay, own, in_sem):
    rows, width = x_ref.shape[0], cb.shape[-1]
    per = sum(sizes)
    subdim = cb.shape[0] // per
    base = xs.shape[1] - per * subdim
    starts = [sum(sizes[:g]) for g in range(len(sizes))]
    groups = range(len(sizes))
    half = n // 2
    folds = n % 2 == 0
    me = lax.axis_index("rows")
    twin = lax.rem(me + half, n)
    near = lax.div(me, half) * half

    barrier = pltpu.get_barrier_semaphore()

    def greet(k, _):
        pl.semaphore_signal(barrier, inc=1, device_id={"rows": lax.rem(me + k, n)},
                            device_id_type=MESH)
        return 0

    lax.fori_loop(1, n, greet, 0, unroll=n <= 8)
    loads = [pltpu.make_async_copy(x_hbm, x_ref, in_sem.at[0]),
             pltpu.make_async_copy(c_hbm, c_ref, in_sem.at[1]),
             pltpu.make_async_copy(cb_hbm.at[me], cb, in_sem.at[2])]
    for load in loads:
        load.start()
    loads[0].wait()
    flipped = x_ref[...].astype(jnp.float32).T
    for j in range(n):
        at = j * per * subdim
        xs[j, base:, :] = flipped[at:at + per * subdim]
    loads[1].wait()
    labels = c_ref[...].astype(jnp.float32).T
    for j in range(n):
        xs[j, :per, :] = labels[j * per:(j + 1) * per]
        if base > per:
            xs[j, per:base, :] = jnp.zeros((base - per, rows), jnp.float32)
    xr[me] = xs[me]
    loads[2].wait()
    pl.semaphore_wait(barrier, n - 1)

    def piece(g):
        first = 0 if g == 0 else base + starts[g] * subdim
        return pl.ds(first, base + (starts[g] + sizes[g]) * subdim - first)

    def lines(g):
        return pl.ds(starts[g] * subdim, sizes[g] * subdim)

    def block(source, target, g):
        return pltpu.make_async_remote_copy(
            src_ref=xs.at[target, piece(g)], dst_ref=xr.at[source, piece(g)],
            send_sem=send_x.at[g, target], recv_sem=recv_x.at[g, source],
            device_id={"rows": target}, device_id_type=MESH)

    def result(source, target, g):
        return pltpu.make_async_remote_copy(
            src_ref=res.at[lines(g)], dst_ref=o_ref.at[source, lines(g)],
            send_sem=send_o.at[g, target], recv_sem=recv_o.at[g, source],
            device_id={"rows": target}, device_id_type=MESH)

    def passed(target, g):
        return pltpu.make_async_remote_copy(
            src_ref=o_ref.at[twin, lines(g)], dst_ref=o_ref.at[twin, lines(g)],
            send_sem=relay.at[g, target], recv_sem=recv_o.at[g, twin],
            device_id={"rows": target}, device_id_type=MESH)

    def kept(g):
        return pltpu.make_async_copy(res.at[lines(g)], o_ref.at[me, lines(g)], own.at[g])

    def each_peer(act):
        def body(k, _):
            act(lax.rem(me + k, n))
            return 0
        if n <= 8:
            for k in sorted(range(1, n), key=lambda k: abs(2 * k - n)):
                body(k, 0)
        else:
            lax.fori_loop(1, n, body, 0)

    def each_near(act):
        def body(k, _):
            act(near + lax.rem(me - near + k, half))
            return 0
        lax.fori_loop(1, half, body, 0, unroll=n <= 8)

    for g in groups:
        each_peer(lambda p, g=g: block(me, p, g).start())

    number = lax.broadcasted_iota(jnp.int32, (width, tile * rows), 0).astype(jnp.float32)
    ones = jnp.ones((8, tile * rows), jnp.float32)

    def over_tiles(step):
        if n == tile:
            return step(0)
        return lax.fori_loop(
            0, n // tile, lambda t, total: total + step(t),
            jnp.zeros((subdim + 8, width), jnp.float32))

    def reduce_rows(points, weights):
        return lax.dot_general(points, weights, (((1,), (1,)), ((), ())),
                               preferred_element_type=jnp.float32)

    def split(value):
        high = value.astype(jnp.bfloat16).astype(jnp.float32)
        middle = (value - high).astype(jnp.bfloat16).astype(jnp.float32)
        return [high, middle, value - high - middle]

    def train(m, _):
        line = pl.multiple_of(m * subdim, subdim)

        def columns(t):
            parts = [xr[t * tile + s, pl.ds(base + line, subdim), :] for s in range(tile)]
            full = jnp.concatenate(parts, axis=1)
            return jnp.concatenate([full, ones], axis=0)

        def first(t):
            code = jnp.concatenate(
                [xr[t * tile + s, pl.ds(m, 1), :] for s in range(tile)], axis=1)
            onehot = (number == code).astype(jnp.float32).astype(jnp.bfloat16)
            return reduce_rows(columns(t).astype(jnp.bfloat16), onehot)

        total = over_tiles(first)
        before = cb[pl.ds(line, subdim), :]
        book = (total[:subdim] + lam * before) / (total[subdim:subdim + 1] + lam)
        scale = 1.4426950408889634
        slope = (2.0 * scale) * book.astype(jnp.bfloat16).astype(jnp.float32)
        norm = -scale * jnp.sum(book * book, axis=0, keepdims=True)
        center = jnp.concatenate(
            split(slope) + split(norm) + [jnp.zeros((5, width), jnp.float32)],
            axis=0).T.astype(jnp.bfloat16)

        def second(t):
            full = columns(t)
            points = jnp.concatenate([full[:subdim]] * 2 + [full], axis=0).astype(jnp.bfloat16)
            scores = jnp.dot(center, points, preferred_element_type=jnp.float32)
            top = jnp.max(scores, axis=0, keepdims=True)
            raised = jnp.exp2(scores - top)
            share = 1.0 / jnp.sum(raised, axis=0, keepdims=True)
            scaled = full * share
            high = scaled.astype(jnp.bfloat16).astype(jnp.float32)
            both = jnp.concatenate([high, scaled - high], axis=0).astype(jnp.bfloat16)
            pair = reduce_rows(both, raised.astype(jnp.bfloat16))
            return pair[:subdim + 8] + pair[subdim + 8:]

        total = over_tiles(second)
        res[pl.ds(line, subdim), :] = (
            (total[:subdim] + lam * book) / (total[subdim:subdim + 1] + lam))
        return 0

    def forward(g):
        result(twin, twin, g).wait_recv()
        each_near(lambda p: passed(p, g).start())

    for g in groups:
        each_peer(lambda p, g=g: block(p, p, g).wait_recv())
        def several(i, _, g=g):
            for u in range(min(4, sizes[g])):
                train(starts[g] + i * min(4, sizes[g]) + u, 0)
            return 0
        lax.fori_loop(0, sizes[g] // min(4, sizes[g]), several, 0)
        if direct[g] or not folds:
            each_peer(lambda p, g=g: result(me, p, g).start())
        else:
            result(me, twin, g).start()
            each_near(lambda p, g=g: result(me, p, g).start())
        kept(g).start()
        if g > 0 and not direct[g - 1] and folds:
            forward(g - 1)
    if not direct[-1] and folds:
        forward(len(sizes) - 1)

    for g in groups:
        each_peer(lambda p, g=g: block(me, p, g).wait_send())
        if direct[g] or not folds:
            each_peer(lambda p, g=g: result(me, p, g).wait_send())
            each_peer(lambda p, g=g: result(p, p, g).wait_recv())
        else:
            result(me, twin, g).wait_send()
            each_near(lambda p, g=g: result(me, p, g).wait_send())
            each_near(lambda p, g=g: passed(p, g).wait_send())
            each_near(lambda p, g=g: result(p, p, g).wait_recv())

            def across(p, g=g):
                q = lax.rem(p + half, n)
                result(q, q, g).wait_recv()

            each_near(across)
        kept(g).wait()


def shards(residuals, codes, codebook):
    rows = residuals.shape[0]
    local, subdim, width = codebook.shape
    n = lax.axis_size("rows")
    per = local // n
    parts = 4 if per % 4 == 0 else 1
    sizes = (per // parts,) * parts
    direct = (False,) * (parts - 1) + (True,)
    lam = rows * n / (8.0 * width)
    tile = min(n, 8)
    base = -(-per // 8) * 8
    held = base + per * subdim
    shape = (n, per * subdim, width)
    out = pl.pallas_call(
        functools.partial(kernel, n, sizes, direct, lam, tile),
        out_shape=pltpu.VMEM(shape, jnp.float32),
        in_specs=[pl.BlockSpec(memory_space=pl.ANY)] * 3,
        out_specs=pl.BlockSpec(memory_space=pltpu.VMEM),
        scratch_shapes=[
            pltpu.VMEM(residuals.shape, residuals.dtype),
            pltpu.VMEM(codes.shape, codes.dtype),
            pltpu.VMEM((n, held, rows), jnp.float32),
            pltpu.VMEM((n, held, rows), jnp.float32),
            pltpu.VMEM((per * subdim, width), jnp.float32),
            pltpu.VMEM((per * subdim, width), jnp.float32),
            pltpu.SemaphoreType.DMA((parts, n)),
            pltpu.SemaphoreType.DMA((parts, n)),
            pltpu.SemaphoreType.DMA((parts, n)),
            pltpu.SemaphoreType.DMA((parts, n)),
            pltpu.SemaphoreType.DMA((parts, n)),
            pltpu.SemaphoreType.DMA((parts,)),
            pltpu.SemaphoreType.DMA((3,)),
        ],
        compiler_params=pltpu.CompilerParams(collective_id=0, has_side_effects=True),
        name="lloyd",
    )(residuals, codes, codebook.reshape(shape))
    return out.reshape(local, subdim, width)


def solution(mesh):
    in_specs = (
        P(("groups", "rows"), "sub"),
        P(("groups", "rows"), "sub"),
        P(("groups", "sub"), None, None),
    )
    out_specs = P(("groups", "sub"), None, None)
    return jax.shard_map(shards, mesh=mesh, in_specs=in_specs, out_specs=out_specs, check_vma=False)
```
